32 devices in a mesh: outer: 2 (over core), rep: 4 (over y, x), exp: 4 (over z).
Axes of the slice: x: 2, y: 2, z: 4, core: 2. Of those that a mesh axis runs over, the one named last changes fastest.
Arguments:
- saved_hidden: bfloat16 [2, 4, 512, 512], P('outer', 'rep', 'exp'), may hold values from -6 to 6
- routed_grad: bfloat16 [2, 4, 512, 2048], P('outer', 'rep', 'exp'), may hold values from -0.19921875 to 0.19921875
- expert_counts: int32 [2, 4, 8], P('outer', 'rep', 'exp'), may hold values from 0 to 128, as said below
- block_starts: int32 [2, 4, 8], P('outer', 'rep', 'exp'), may hold values from 0 to 1
- master_weights: float32 [8, 2048, 512], P('exp', 'rep', 'outer'), may hold values from -0.0125 to 0.0125
- first_moment: float32 [8, 2048, 512], P('exp', 'rep', 'outer'), may hold values from -0.9 to 0.9
- second_moment: float32 [8, 2048, 512], P('exp', 'rep', 'outer'), may hold values from 0.01 to 1
Outputs:
- new_master: float32 [8, 2048, 512], P('exp', 'rep', 'outer')
- new_first: float32 [8, 2048, 512], P('exp', 'rep', 'outer')
- new_second: float32 [8, 2048, 512], P('exp', 'rep', 'outer')
- new_weights: bfloat16 [8, 2048, 512], P('exp')
The draws below stay inside these ranges and needn't reach their ends.
Inputs may be any that keep to these rules, and one draw needn't show every extreme that they name: On each device, the rows of its local expert e are rows 128 * block_starts[e] to 128 * block_starts[e] + expert_counts[e] - 1 of its 128 expert-side rows; the local experts come in increasing order of e, each in whole blocks of 128 rows of its own that no other expert touches, all within the device's 1 block; other rows belong to no expert. In every draw some device gives all its 1 block to one expert.
All inputs are finite; a program needn't handle non-finite values.
Results may differ from the reference program's by a relative error of at most 0.015.
Values may be sent and summed in bfloat16 or wider, within the bound.
No kernel may reach another device: no remote copies, remote signals or barrier semaphores. Data moves between devices by JAX's collectives and lax.ppermute only.
A program may use at most 64 MiB of HBM per device.

```python
import math
import jax
import jax.numpy as jnp
from jax import lax

D = 2048
FF = 512
EXP_DEV = 2
CAP = 32
BLOCK = 128
EXPERTS = 8
N_OUTER = 2
N_REP = 4
N_EXP = 4


def expert_layout(key):
    block_total = N_EXP * CAP // BLOCK
    key_raw, key_gap, key_extra = jax.random.split(jax.random.fold_in(key, 7), 3)
    shape = (N_OUTER, N_REP, N_EXP, EXP_DEV)
    base = jax.random.randint(key_raw, shape, 0, 4)
    weights_raw = base * base
    summed = jnp.sum(weights_raw, axis=-1, keepdims=True)
    blocks_each = weights_raw * block_total // jnp.maximum(summed, 9)
    leading = jnp.zeros((EXP_DEV,), jnp.int32).at[0].set(block_total)
    blocks_each = blocks_each.at[0, 0, 0].set(leading)
    slack = block_total - jnp.sum(blocks_each, axis=-1, keepdims=True)
    gap_raw = jax.random.randint(key_gap, shape, 0, 4)
    gaps = gap_raw * slack // jnp.maximum(jnp.sum(gap_raw, axis=-1, keepdims=True), 1)
    starts = jnp.cumsum(gaps + blocks_each, axis=-1) - blocks_each
    extra = jax.random.randint(key_extra, shape, 0, BLOCK)
    extra = extra.at[0, 0, 0, 0].set(BLOCK - 1)
    counts = jnp.where(blocks_each > 0, (blocks_each - 1) * BLOCK + 1 + extra, 0)
    counts = counts.reshape(N_OUTER, N_REP, N_EXP * EXP_DEV).astype(jnp.int32)
    starts = starts.reshape(N_OUTER, N_REP, N_EXP * EXP_DEV).astype(jnp.int32)
    return (counts, starts)


def draw_expert_counts(key, part):
    return expert_layout(key)[0]


def draw_block_starts(key, part):
    return expert_layout(key)[1]


def raised(array, stream_key, source, target, blocks, factor):
    def block_of(axis_at):
        return (jnp.arange(array.shape[axis_at]) // (array.shape[axis_at] // blocks)).reshape((-1,) + (1,) * (array.ndim - 1 - axis_at))

    near = jax.random.permutation(stream_key, blocks)[block_of(target)]
    second = (block_of(target) + blocks // 2) % blocks
    return jnp.where((block_of(source) == near) | (block_of(source) == second), factor * array, array)


def block_scale(rng, extent, shards, least, largest):
    def one(dim, blocks):
        heights = jax.random.uniform(jax.random.fold_in(jax.random.fold_in(rng, 6), dim), (blocks,), jnp.float32, least / len(shards), largest / len(shards))
        return jnp.repeat(jnp.exp(heights), extent[dim] // blocks).reshape((-1,) + (1,) * (len(extent) - dim - 1))

    gain = one(*shards[0])
    for cut in shards[1:]:
        gain = gain * one(*cut)
    return gain


def centred(key, extent, spread, reach, shards=(), kind=jnp.bfloat16):
    factor_of = block_scale(key, extent, shards, -0.22, 0.18) if shards else 1.0
    result = jax.random.normal(key, extent, jnp.float32) * spread * factor_of
    return jnp.minimum(jnp.maximum(result, -reach), reach).astype(kind)


def bell_draw_with(own_key, extent, spread, limit, pieces, heavy, held_as=jnp.bfloat16):
    array = spread * jax.random.normal(own_key, extent, jnp.float32)
    if pieces:
        array = array * block_scale(own_key, extent, pieces, -0.22, 0.18)
    return jnp.clip(raised(array, jax.random.fold_in(own_key, 3), *heavy), -limit, limit).astype(held_as)


def setup_inputs(seed: int = 0) -> dict:
    splits = jax.random.split(jax.random.key(seed), 8)
    return {
        "saved_hidden": centred(splits[0], (N_OUTER, N_REP, N_EXP * N_EXP * CAP, FF), 1.0, 6.0, ((0, 2), (1, 4), (2, 4))),
        "routed_grad": bell_draw_with(splits[1], (N_OUTER, N_REP, N_EXP * N_EXP * CAP, D), 0.03125, 0.19921875, ((0, 2), (1, 4), (2, 4)), (1, 3, 4, 2.0)),
        "expert_counts": draw_expert_counts(jax.random.fold_in(splits[7], 71), 0),
        "block_starts": draw_block_starts(jax.random.fold_in(splits[7], 71), 0),
        "master_weights": centred(splits[4], (EXPERTS, D, FF), 0.005, 0.0125, ((0, 4), (1, 4), (2, 2)), jnp.float32),
        "first_moment": centred(splits[5], (EXPERTS, D, FF), 0.15, 0.9, ((0, 4), (1, 4), (2, 2)), jnp.float32),
        "second_moment": jnp.clip(jnp.exp(math.log(1.0) - 4.6051702 * jax.random.uniform(splits[6], (EXPERTS, D, FF), jnp.float32) ** block_scale(splits[6], (EXPERTS, D, FF), ((0, 4), (1, 4), (2, 2)), -0.2, 0.2)), 0.01, 1.0),
    }


beta_one = 0.9
beta_two = 0.95
learn_rate = 0.001
decay_rate = 0.1
epsilon = 1e-08
correct_one = 0.9999734386011124
correct_two = 0.994079470779666

def adamw(grad_part, master, moment_one, moment_two):
    new_one = beta_one * moment_one + (1.0 - beta_one) * grad_part
    new_two = beta_two * moment_two + (1.0 - beta_two) * grad_part * grad_part
    update = new_one / correct_one / (jnp.sqrt(new_two / correct_two) + epsilon)
    new_master = master - learn_rate * (update + decay_rate * master)
    return (new_master, new_one, new_two)

def device_partial(hidden, grads, counts, starts):
    positions = jnp.arange(hidden.shape[0], dtype=jnp.int32)
    lower_row = starts * BLOCK
    upper_row = lower_row + counts
    member = (positions[None, :] >= lower_row[:, None]) & (positions[None, :] < upper_row[:, None])
    masked = jnp.where(member[:, :, None], hidden.astype(jnp.float32)[None, :, :], 0.0)
    return jnp.einsum('rd,erf->edf', grads.astype(jnp.float32), masked)

def reference(saved_hidden, routed_grad, expert_counts, block_starts, master_weights, first_moment, second_moment):
    replicas = N_OUTER * N_REP
    row_total = N_EXP * CAP
    hidden_all = saved_hidden.reshape(replicas, N_EXP, row_total, FF)
    grads_all = routed_grad.reshape(replicas, N_EXP, N_EXP, CAP, D)
    counts_all = expert_counts.reshape(replicas, N_EXP, EXP_DEV)
    starts_all = block_starts.reshape(replicas, N_EXP, EXP_DEV)

    def group(owner):
        hidden_group = lax.dynamic_index_in_dim(hidden_all, owner, 1, keepdims=False)
        grads_group = lax.dynamic_index_in_dim(grads_all, owner, 2, keepdims=False).reshape(replicas, row_total, D)
        counts_group = lax.dynamic_index_in_dim(counts_all, owner, 1, keepdims=False)
        starts_group = lax.dynamic_index_in_dim(starts_all, owner, 1, keepdims=False)

        def add(summed, item):
            partial_value = device_partial(item[0], item[1], item[2], item[3])
            rounded = lax.optimization_barrier(partial_value.astype(jnp.bfloat16))
            return (summed + rounded.astype(jnp.float32), None)
        summed, unused = lax.scan(add, jnp.zeros((EXP_DEV, D, FF), jnp.float32), (hidden_group, grads_group, counts_group, starts_group))
        return summed
    grouped = lax.map(group, jnp.arange(N_EXP, dtype=jnp.int32))
    grad_full = grouped.reshape(N_EXP * EXP_DEV, D, FF)
    new_master, new_first, new_second = adamw(grad_full, master_weights, first_moment, second_moment)
    return (new_master, new_first, new_second, new_master.astype(jnp.bfloat16))
```

```python
import jax
import jax.numpy as jnp
from jax import lax
from jax.experimental import pallas as pl
from jax.experimental.pallas import tpu as pltpu
from jax.sharding import PartitionSpec as P

BLOCK = 128
FLAG_ROWS = 16

beta_one = 0.9
beta_two = 0.95
learn_rate = 0.001
decay_rate = 0.1
epsilon = 1e-08
correct_one = 0.9999734386011124
correct_two = 0.994079470779666


def adamw(grad_part, master, moment_one, moment_two):
    new_one = beta_one * moment_one + (1.0 - beta_one) * grad_part
    new_two = beta_two * moment_two + (1.0 - beta_two) * grad_part * grad_part
    update = new_one / correct_one / (jnp.sqrt(new_two / correct_two) + epsilon)
    new_master = master - learn_rate * (update + decay_rate * master)
    return (new_master, new_one, new_two)


def split_experts(flat_terms, experts_here, hidden_units):
    return jnp.stack(
        [
            flat_terms[:, index * hidden_units : (index + 1) * hidden_units]
            for index in range(experts_here)
        ],
        axis=0,
    )


def general_body(
    saved_hidden,
    routed_grad,
    expert_counts,
    block_starts,
    master_weights,
    first_moment,
    second_moment,
):
    model_width = routed_grad.shape[-1]
    hidden_units = saved_hidden.shape[-1]
    outgoing = routed_grad.reshape(-1, model_width)
    arrived = lax.all_to_all(outgoing, "exp", split_axis=0, concat_axis=0, tiled=True)
    hidden = saved_hidden.reshape(-1, hidden_units)
    row_total = hidden.shape[0]
    counts_local = expert_counts.reshape(-1)
    lower_row = block_starts.reshape(-1) * BLOCK
    upper_row = lower_row + counts_local
    experts_here = counts_local.shape[0]
    positions = lax.iota(jnp.int32, row_total)
    member = (positions[:, None] >= lower_row[None, :]) & (positions[:, None] < upper_row[None, :])
    masked = jnp.concatenate(
        [
            jnp.where(member[:, index : index + 1], hidden, jnp.zeros((), jnp.bfloat16))
            for index in range(experts_here)
        ],
        axis=1,
    )
    whole = split_experts(
        lax.dot_general(
            arrived, masked, (((0,), (0,)), ((), ())), preferred_element_type=jnp.float32
        ),
        experts_here,
        hidden_units,
    )
    inner = lax.psum_scatter(whole.astype(jnp.bfloat16), "outer", scatter_dimension=2, tiled=True)
    grad_part = lax.psum_scatter(inner, "rep", scatter_dimension=1, tiled=True).astype(jnp.float32)
    new_master, new_first, new_second = adamw(
        grad_part, master_weights, first_moment, second_moment
    )
    updated = new_master.astype(jnp.bfloat16)
    along = lax.all_gather(updated, "rep", axis=1, tiled=True)
    new_weights = lax.all_gather(along, "outer", axis=2, tiled=True)
    return (new_master, new_first, new_second, new_weights)


def grad_kernel(n_exp, where_ref, *refs):
    rows = refs[: 2 * n_exp]
    hidden = refs[2 * n_exp : 2 * n_exp + 4]
    master, first, second = refs[2 * n_exp + 4 : 2 * n_exp + 7]
    out_master, out_first, out_second, out_weights = refs[2 * n_exp + 7 : 2 * n_exp + 11]
    lhs, rhs = refs[2 * n_exp + 11 :]
    experts = rhs.shape[0]
    piece = rows[0].shape[0]
    slots = piece // 4
    block = hidden[0].shape[0] // 2

    @pl.when((pl.program_id(0) == 0) & (pl.program_id(1) == 0))
    def _():
        for index, ref in enumerate(rows):
            lhs[index * piece : (index + 1) * piece, :] = ref[...]
        for side in range(2):
            for hop in range(n_exp):
                source = lax.rem(where_ref[0] + n_exp - hop, n_exp)
                for near in range(4):
                    start = pl.multiple_of(side * block + source * slots, slots)
                    part = hidden[near][pl.ds(start, slots), :]
                    at = ((side * n_exp + hop) * 4 + near) * slots
                    for e in range(experts):
                        flag_at = side * block + BLOCK
                        flag = hidden[near][flag_at : flag_at + 16, :][e : e + 1, :]
                        rhs[e, at : at + slots, :] = jnp.where(
                            flag.astype(jnp.float32) > 0.5, part, jnp.zeros_like(part)
                        )

    e = pl.program_id(0)
    tile = master.shape[1]
    at = pl.multiple_of(pl.program_id(1) * tile, tile)
    grad = lax.dot_general(
        lhs[:, pl.ds(at, tile)],
        rhs[e],
        (((0,), (0,)), ((), ())),
        preferred_element_type=jnp.float32,
    )
    new_master, new_first, new_second = adamw(grad, master[0], first[0], second[0])
    out_master[0] = new_master
    out_first[0] = new_first
    out_second[0] = new_second
    out_weights[0] = new_master.astype(jnp.bfloat16)


def grad_and_update(n_exp, where, rows, hidden, master, first, second):
    experts, width, units = master.shape
    tile = min(width, 128)
    total = sum(piece.shape[0] for piece in rows)

    def fixed(array):
        return pl.BlockSpec(array.shape, lambda e, i, w: (0,) * array.ndim)

    shard = pl.BlockSpec((1, tile, units), lambda e, i, w: (e, i, 0))
    return pl.pallas_call(
        lambda *refs: grad_kernel(n_exp, *refs),
        grid_spec=pltpu.PrefetchScalarGridSpec(
            num_scalar_prefetch=1,
            grid=(experts, width // tile),
            in_specs=[fixed(a) for a in (*rows, *hidden)] + [shard] * 3,
            out_specs=[shard] * 4,
            scratch_shapes=[
                pltpu.VMEM((total, width), jnp.bfloat16),
                pltpu.VMEM((experts, total, units), jnp.bfloat16),
            ],
        ),
        out_shape=[jax.ShapeDtypeStruct(master.shape, jnp.float32)] * 3
        + [jax.ShapeDtypeStruct(master.shape, jnp.bfloat16)],
        name="grad_and_update",
    )(where, *rows, *hidden, master, first, second)


def place_kernel(where_ref, *refs):
    out = refs[-1]
    swap = where_ref[1] == 1
    units = refs[0].shape[-1]
    near = pl.program_id(1)
    for j in range(4):

        @pl.when(near == j)
        def _():
            mine, other = refs[j][0], refs[4 + j][0]
            out[0, :, :units] = jnp.where(swap, other, mine)
            out[0, :, units:] = jnp.where(swap, mine, other)


def place_weights(where, mine, other):
    experts, width, units = mine[0].shape
    piece = pl.BlockSpec((1, width, units), lambda e, j, w: (e, 0, 0))
    return pl.pallas_call(
        place_kernel,
        grid_spec=pltpu.PrefetchScalarGridSpec(
            num_scalar_prefetch=1,
            grid=(experts, 4),
            in_specs=[piece] * 8,
            out_specs=pl.BlockSpec((1, width, 2 * units), lambda e, j, w: (e, w[2] ^ j, 0)),
        ),
        out_shape=jax.ShapeDtypeStruct((experts, 4 * width, 2 * units), jnp.bfloat16),
        name="place_weights",
    )(where, *mine, *other)


def swap_outer(array):
    return lax.ppermute(array, "outer", [(0, 1), (1, 0)])


def to_near(array, j):
    return lax.ppermute(array, "rep", [(i, i ^ j) for i in range(4)])


def small_body(n_exp, saved_hidden, routed_grad, expert_counts, block_starts, master, first, second):
    outer = lax.axis_index("outer")
    rep = lax.axis_index("rep")
    exp = lax.axis_index("exp")
    where = jnp.stack([exp, outer, rep]).astype(jnp.int32)
    grads = routed_grad.reshape(-1, routed_grad.shape[-1])
    hidden = saved_hidden.reshape(-1, saved_hidden.shape[-1])
    counts = expert_counts.reshape(-1)
    starts = block_starts.reshape(-1)
    experts, width, units = master.shape
    slots = grads.shape[0] // n_exp

    position = lax.broadcasted_iota(jnp.int32, hidden.shape, 0)
    kept = jnp.zeros(hidden.shape, jnp.bool_)
    flags = jnp.zeros((FLAG_ROWS, hidden.shape[1]), jnp.bool_)
    flag_row = lax.broadcasted_iota(jnp.int32, flags.shape, 0)
    for e in range(experts):
        low = starts[e] * BLOCK
        kept = kept | ((position >= low) & (position < low + counts[e]))
        flags = flags | ((flag_row == e) & (starts[e] == 0) & (counts[e] > 0))
    zero = jnp.zeros((), jnp.bfloat16)
    marked = jnp.concatenate(
        [jnp.where(kept, hidden, zero), flags.astype(jnp.bfloat16)], axis=0
    )
    own_half = lax.dynamic_slice_in_dim(marked, outer * units, units, 1)
    other_half = lax.dynamic_slice_in_dim(marked, (1 - outer) * units, units, 1)
    both = jnp.concatenate([own_half, swap_outer(other_half)], axis=0)
    hidden_near = [both] + [to_near(both, j) for j in (1, 2, 3)]

    slices = [lax.dynamic_slice_in_dim(grads, (rep ^ j) * width, width, 1) for j in range(4)]
    slices = [slices[0]] + [to_near(slices[j], j) for j in (1, 2, 3)]
    rows = []
    for hop in range(n_exp):
        target = lax.rem(exp + hop, n_exp)
        piece = jnp.concatenate(
            [lax.dynamic_slice_in_dim(s, target * slots, slots, 0) for s in slices], axis=0
        )
        if hop:
            piece = lax.ppermute(piece, "exp", [(i, (i + hop) % n_exp) for i in range(n_exp)])
        rows.append(piece)
    rows = rows + [swap_outer(piece) for piece in rows]

    new_master, new_first, new_second, shard = grad_and_update(
        n_exp, where, rows, hidden_near, master, first, second
    )

    along_x = to_near(shard, 1)
    along_y = to_near(shard, 2)
    relay = jnp.where(outer == 0, along_x, along_y)
    far = lax.ppermute(
        relay,
        ("outer", "rep"),
        [(o * 4 + i, o * 4 + (i ^ (2 if o == 0 else 1))) for o in range(2) for i in range(4)],
    )
    mine = [shard, along_x, along_y, far]
    other = [swap_outer(piece) for piece in mine]
    return (new_master, new_first, new_second, place_weights(where, mine, other))


def solution(mesh):
    in_specs = (
        P("outer", "rep", "exp", None),
        P("outer", "rep", "exp", None),
        P("outer", "rep", "exp"),
        P("outer", "rep", "exp"),
        P("exp", "rep", "outer"),
        P("exp", "rep", "outer"),
        P("exp", "rep", "outer"),
    )
    out_specs = (
        P("exp", "rep", "outer"),
        P("exp", "rep", "outer"),
        P("exp", "rep", "outer"),
        P("exp", None, None),
    )

    def body(saved_hidden, *rest):
        n_exp = mesh.shape["exp"]
        one_block = saved_hidden.shape[2] == BLOCK
        if mesh.shape["outer"] == 2 and mesh.shape["rep"] == 4 and one_block:
            return small_body(n_exp, saved_hidden, *rest)
        return general_body(saved_hidden, *rest)

    return jax.shard_map(body, mesh=mesh, in_specs=in_specs, out_specs=out_specs, check_vma=False)
```
